512 devices in a mesh: mpo: 16 (over y, x), sector: 32 (over z, core).
Axes of the slice: x: 4, y: 4, z: 16, core: 2. Of those that a mesh axis runs over, the one named last changes fastest.
Arguments:
- wavefunction: bfloat16 [128, 512, 512], P('sector'), may hold values from -6 to 6
- left_env: bfloat16 [16, 128, 512, 512], P('mpo', 'sector'), may hold values from -0.375 to 0.375
- right_env: bfloat16 [16, 128, 512, 512], P('mpo', 'sector'), may hold values from -0.0625 to 0.0625
- mpo_mask: int32 [16, 128], P('mpo', 'sector'), may hold values 0 or 1
- block_size: int32 [128], P('sector'), may hold values from 64 to 512, as said below
- route_owner: int32 [16, 128, 8], P('mpo', 'sector'), may hold values from 0 to 31, all different within a row; in each aligned block of 4 rows (0 to 3, 4 to 7, ..., all dimensions but the last counted through in order) at most 2 rows name the same one
- route_block: int32 [16, 128, 8], P('mpo', 'sector'), may hold values from 0 to 3
Outputs:
- sigma_right: bfloat16 [128, 512, 512], P('sector', 'mpo')
The draws below stay inside these ranges and needn't reach their ends.
Inputs may be any that keep to these rules, and one draw needn't show every extreme that they name: `block_size`: some block in every draw has all 512 states live. `route_owner`: each row (m, b) names 8 different owners. Among the 4 rows of one device (one m and the blocks of one sector owner) no owner is named more than 2 times, and in some device's rows some owner is named exactly 2 times; every owner is named somewhere.
All inputs are finite; a program needn't handle non-finite values. No bound on the sum of `mpo_mask` on one device may be relied on, other than what follows from the above.
Results may differ from the reference program's by a relative error of at most 0.014.
Values may be sent and summed in bfloat16 or wider, within the bound.
A program may use at most 64 MiB of HBM per device.

```python
import math
import jax
import jax.numpy as jnp
import numpy as np
from jax import lax

STATES = 512
NB_DEV = 4
ROW_GROUPS = 4
COL_PARTS = 2
PIECES = 8
CAP = 2
NBLOCKS = 128
BONDS = 16
N_MPO = 16
N_SECTOR = 32


def draw_block_size(key, part):
    key_sizes, key_pick = jax.random.split(jax.random.fold_in(key, 17))
    drawn = jax.random.randint(key_sizes, (NBLOCKS,), STATES // 8, STATES + 1, dtype=jnp.int32)
    chosen = jax.random.randint(key_pick, (), 0, NBLOCKS, dtype=jnp.int32)
    return jnp.where(jnp.arange(NBLOCKS, dtype=jnp.int32) == chosen, STATES, drawn).astype(jnp.int32)


def plant(values, own_key, low, largest):
    longest = values.shape.index(max(values.shape))
    spots = []
    for shift in (0, 1):
        where = [jax.random.randint(jax.random.fold_in(own_key, axis), (), 0, length) for axis, length in enumerate(values.shape)]
        where[longest] = (where[longest] + shift) % values.shape[longest]
        spots.append(tuple(where))
    return values.at[spots[0]].set(low).at[spots[1]].set(largest)


def spiked(values, key, source, target, blocks, factor):
    def block_of(position):
        return (jnp.arange(values.shape[position]) // (values.shape[position] // blocks)).reshape((-1,) + (1,) * (values.ndim - 1 - position))

    near = jax.random.permutation(key, blocks)[block_of(target)]
    other_side = (block_of(target) + blocks // 2) % blocks
    return jnp.where((block_of(source) == near) | (block_of(source) == other_side), factor * values, values)


def steps_of(stream_key, dims, cuts, low, largest):
    def one(position, parts):
        heights = jax.random.uniform(jax.random.fold_in(jax.random.fold_in(stream_key, 6), position), (parts,), jnp.float32, low / len(cuts), largest / len(cuts))
        return jnp.repeat(jnp.exp(heights), dims[position] // parts).reshape((-1,) + (1,) * (len(dims) - position - 1))

    factor_of = one(*cuts[0])
    for cut in cuts[1:]:
        factor_of = factor_of * one(*cut)
    return factor_of


def routed_block(key, own, number, rows, number_of, top, limit, skew):
    sequence = jax.random.permutation(key, number_of)
    heavy_load, common = load_shares(number_of, rows * top, limit, skew, True), load_shares(number_of, rows * top, limit, skew, False)
    places = jnp.arange(number_of)

    def named(tallies, rotation):
        used = int((tallies > 0).sum())
        fixed = max(1, used // 4)
        moved = fixed + (places - fixed + rotation * (used - fixed)) % max(1, number_of - fixed)
        return jnp.zeros((number_of,), jnp.int32).at[sequence[jnp.where(places < fixed, places, moved)]].set(jnp.asarray(tallies, jnp.int32))

    tallies = jnp.where(number % 4 == 0, named(heavy_load, number // 4), named(common, number - number // 4 - 1))
    mixed = jax.random.permutation(jax.random.fold_in(own, 3), number_of)
    source_of, taker = mixed[0:number_of // 2 * 2:2], mixed[1:number_of // 2 * 2:2]
    slack = jnp.minimum(tallies[source_of] - 1, limit - tallies[taker]) // 2
    slack = jnp.where((source_of == sequence[0]) | (taker == sequence[0]) | (tallies[taker] == 0), 0, jnp.maximum(slack, 0))
    moved = jax.random.randint(jax.random.fold_in(own, 4), (number_of // 2,), 0, 1 << 20) % (slack + 1)
    tallies = tallies.at[source_of].add(-moved).at[taker].add(moved)
    items = jnp.searchsorted(jnp.cumsum(tallies), jnp.arange(rows * top), side="right").astype(jnp.int32)
    listing = items.reshape(top, rows).T
    listing = listing[jax.random.permutation(jax.random.fold_in(own, 1), rows)]
    rotation = jax.random.randint(jax.random.fold_in(own, 2), (rows, 1), 0, top)
    return jnp.take_along_axis(listing, (jnp.arange(top)[None, :] + rotation) % top, axis=1)


def load_shares(amount, total, most, lean, full):
    weights = [(1 << 20) // math.isqrt(rank ** lean) + 1 for rank in range(1, amount + 1)]
    largest = most if full else min(most, max(-(-total // amount), total * weights[0] // sum(weights)))
    least = 1 if total - largest >= amount - 1 else 0
    holding, spare = [largest] + [least] * (amount - 1), total - largest - least * (amount - 1)
    while spare > 0:
        free = [i for i in range(1, amount) if holding[i] < largest] or [i for i in range(1, amount) if holding[i] < most]
        mass, remaining = sum([weights[i] for i in free]), spare
        for i in free:
            more = min(most - holding[i], max(1, remaining * weights[i] // mass), spare)
            holding[i] = holding[i] + more
            spare = spare - more
    return np.array(holding)


def gaussian(stream_key, extent, scale, bound, cuts=(), held_as=jnp.bfloat16):
    values = scale * jax.random.normal(stream_key, extent, jnp.float32)
    if cuts:
        values = values * steps_of(stream_key, extent, cuts, -0.22, 0.18)
    return jnp.clip(values, -bound, bound).astype(held_as)


def heavy_noise(stream_key, extent, width, most, cuts, heavy, kind=jnp.bfloat16):
    values = width * jax.random.normal(stream_key, extent, jnp.float32)
    if cuts:
        values = values * steps_of(stream_key, extent, cuts, -0.22, 0.18)
    return jnp.clip(spiked(values, jax.random.fold_in(stream_key, 3), *heavy), -most, most).astype(kind)


def setup_inputs(seed: int = 0) -> dict:
    key_list = jax.random.split(jax.random.key(seed), 8)
    wavefunction = gaussian(key_list[0], (NBLOCKS, STATES, STATES), 1.0, 6.0, ((0, 32),))
    left_env = heavy_noise(key_list[1], (BONDS, NBLOCKS, STATES, STATES), STATES ** -0.5, 0.375, ((0, 16), (1, 32)), (0, 2, 16, 2.0))
    right_env = gaussian(key_list[2], (BONDS, NBLOCKS, STATES, STATES), (STATES * BONDS) ** -0.5, 0.0625, ((0, 16), (1, 32)))
    mpo_mask = plant((jax.random.randint(key_list[3], (BONDS, NBLOCKS), 0, 4) < 3).astype(jnp.int32), jax.random.fold_in(key_list[3], 1), 0, 1)
    block_size = draw_block_size(jax.random.fold_in(key_list[7], 71), 0)
    route_owner_keys = jax.random.split(jax.random.fold_in(key_list[5], 1), BONDS * NBLOCKS // NB_DEV)
    route_owner_turns = jax.random.permutation(jax.random.fold_in(key_list[5], 3), BONDS * NBLOCKS // NB_DEV)
    route_owner = jax.vmap(lambda own, number: routed_block(jax.random.fold_in(key_list[5], 2), own, number, NB_DEV, N_SECTOR, PIECES, CAP, 2))(route_owner_keys, route_owner_turns).reshape((BONDS, NBLOCKS, PIECES))
    route_block = plant(jax.random.randint(key_list[6], (BONDS, NBLOCKS, PIECES), 0, NB_DEV), jax.random.fold_in(key_list[6], 1), 0, NB_DEV - 1).astype(jnp.int32)
    return dict(wavefunction=wavefunction, left_env=left_env, right_env=right_env, mpo_mask=mpo_mask, block_size=block_size, route_owner=route_owner, route_block=route_block)


def reference(wavefunction, left_env, right_env, mpo_mask, block_size, route_owner, route_block):
    nblocks = wavefunction.shape[0]
    states = wavefunction.shape[1]
    positions = jnp.arange(states, dtype=jnp.int32)
    live_rows = positions[None, :] < block_size[:, None]
    live_mask = live_rows[:, :, None] & live_rows[:, None, :]
    masked = jnp.where(live_mask, wavefunction, jnp.zeros_like(wavefunction))

    def one_index(running, inputs):
        left_slice, right_slice, mask_slice = inputs
        right_part = jnp.einsum("bij,bkj->bik", masked.astype(jnp.float32), right_slice.astype(jnp.float32)).astype(jnp.bfloat16)
        product = jnp.einsum("bij,bjk->bik", left_slice.astype(jnp.float32), right_part.astype(jnp.float32))
        product = product * mask_slice.astype(jnp.float32)[:, None, None]
        rounded = lax.optimization_barrier(product.astype(jnp.bfloat16))
        return running + rounded.astype(jnp.float32), None

    summed, _ = lax.scan(one_index, jnp.zeros(wavefunction.shape, jnp.float32), (left_env, right_env, mpo_mask))
    sigma_left = jnp.where(live_mask, summed, jnp.zeros_like(summed)).astype(jnp.bfloat16)

    group_rows = states // (N_MPO * ROW_GROUPS)
    width_part = states // COL_PARTS
    pieces = sigma_left.reshape(nblocks, N_MPO, ROW_GROUPS, group_rows, COL_PARTS, width_part)
    pieces = pieces.transpose(1, 0, 2, 4, 3, 5).reshape(N_MPO, nblocks, PIECES, group_rows, width_part)
    target = (route_owner * NB_DEV + route_block).astype(jnp.int32)
    piece_ids = jnp.arange(PIECES, dtype=jnp.int32)[None, None, :]
    mpo_ids = jnp.arange(N_MPO, dtype=jnp.int32)[:, None, None]
    result = jnp.zeros((nblocks, N_MPO, PIECES, group_rows, width_part), jnp.float32)
    result = result.at[target, mpo_ids, piece_ids].add(pieces.astype(jnp.float32))
    result = result.reshape(nblocks, N_MPO, ROW_GROUPS, COL_PARTS, group_rows, width_part)
    result = result.transpose(0, 1, 2, 4, 3, 5).reshape(nblocks, states, states)
    return result.astype(jnp.bfloat16)
```

```python
import functools

import jax
import jax.numpy as jnp
from jax import lax
from jax.experimental import pallas as pl
from jax.experimental.pallas import tpu as pltpu
from jax.sharding import PartitionSpec as P

MESH = pl.DeviceIdType.MESH
F32, BF16, I32 = jnp.float32, jnp.bfloat16, jnp.int32
NB = 4
N = 512
RING = 4
SHARE = 32
W = 128
CHUNKS = 2
NS = 32
SLOT_ROWS = 16


def iota(shape, dim):
    return lax.broadcasted_iota(I32, shape, dim)


def one_hot_rows(chosen, base):
    lane = iota((NS, 128), 1)
    first = jnp.min(jnp.where(chosen, lane, 999), axis=1, keepdims=True)
    last = jnp.max(jnp.where(chosen, lane, -1), axis=1, keepdims=True)
    none = 256.0
    at_first = jnp.sum(jnp.where(lane == first, base, 0), axis=1, keepdims=True).astype(F32)
    at_last = jnp.sum(jnp.where(lane == last, base, 0), axis=1, keepdims=True).astype(F32)
    slot0 = jnp.where(first < 999, at_first, none)
    slot1 = jnp.where(last > first, at_last, none)
    both = jnp.where(lane < 64, slot0, slot1).astype(BF16)
    spread = (iota((NS * SLOT_ROWS, NS), 0) // SLOT_ROWS == iota((NS * SLOT_ROWS, NS), 1)).astype(F32).astype(BF16)
    rows = jnp.dot(spread, both, preferred_element_type=F32)
    inner = iota((NS * SLOT_ROWS, 1), 0) % SLOT_ROWS
    value = jnp.where(inner < 8, rows[:, 0:1], rows[:, 64:65]).astype(I32)
    value = jnp.where(value < 256, value + inner % 8, -1)
    return (iota((NS * SLOT_ROWS, 256), 1) == value).astype(F32).astype(BF16)


def kernel(
    wf_hbm, le_hbm, re_hbm, mask_hbm, size_hbm, owner_hbm, block_hbm,
    out_ref,
    wf, le, re, prod, r1, f1, q, r2, f2, pieces, sbuf, arr, tab, row, place, collect, outv,
    mask_s, size_s, owner_s, block_s,
    load_sem, small_sem, ss1, rs1, ss2, rs2, ssb, rsb, ssm, rsm, out_sem,
):
    m = lax.axis_index("mpo")
    s = lax.axis_index("sector")
    y, x = m // RING, m % RING

    loads = {}

    def load(key, src, dst, sem):
        c = pltpu.make_async_copy(src, dst, sem)
        c.start()
        loads[key] = c

    load("mask", mask_hbm, mask_s, small_sem.at[0])
    load("size", size_hbm, size_s, small_sem.at[1])
    load("owner", owner_hbm, owner_s, small_sem.at[2])
    load("block", block_hbm, block_s, small_sem.at[3])
    for b in range(NB):
        load(("wf", b), wf_hbm.at[b], wf.at[b], load_sem.at[b, 0])
        load(("re", b), re_hbm.at[0, b], re.at[b], load_sem.at[b, 1])
        load(("le", b), le_hbm.at[0, b], le.at[b], load_sem.at[b, 2])

    def ring_device(axis, delta):
        if axis == 0:
            return y * RING + (x + delta + RING) % RING
        return ((y + delta + RING) % RING) * RING + x

    def ring_pos(axis, delta):
        return ((x if axis == 0 else y) + delta + RING) % RING

    barrier = pltpu.get_barrier_semaphore()
    for axis in (0, 1):
        for delta in (1, -1):
            pl.semaphore_signal(barrier, inc=1, device_id={"mpo": ring_device(axis, delta), "sector": s}, device_id_type=MESH)

    @pl.loop(1, NS)
    def _(d):
        pl.semaphore_signal(barrier, inc=1, device_id={"mpo": m, "sector": (s + d) % NS}, device_id_type=MESH)

    for key in ("mask", "size", "owner", "block"):
        loads[key].wait()

    started = []

    def send(src, dst, ss, rs, dev):
        c = pltpu.make_async_remote_copy(
            src_ref=src, dst_ref=dst, send_sem=ss, recv_sem=rs, device_id={"mpo": dev, "sector": s}, device_id_type=MESH
        )
        c.start()
        started.append(c)

    def wait_recv(dst, ss, rs):
        pltpu.make_async_remote_copy(
            src_ref=dst, dst_ref=dst, send_sem=ss, recv_sem=rs, device_id={"mpo": m, "sector": s}, device_id_type=MESH
        ).wait_recv()

    def compute(j, b):
        if j == 0:
            loads[("wf", b)].wait()
            size = size_s[b] * mask_s[0, b]
            live = (iota((N, N), 0) < size) & (iota((N, N), 1) < size)
            wf[b] = jnp.where(live, wf[b], jnp.zeros((), BF16))
            loads[("re", b)].wait()
        rhs = jnp.concatenate([re[b, j * W : (j + 1) * W], re[b, 256 + j * W : 256 + (j + 1) * W]], axis=0)
        right = lax.dot_general(wf[b], rhs, (((1,), (1,)), ((), ())), preferred_element_type=F32).astype(BF16)
        if j == 0:
            loads[("le", b)].wait()
        out = jnp.dot(le[b], right, preferred_element_type=F32).astype(BF16)
        prod[j, 0, b] = out[:, :W].reshape(RING, RING, SHARE, W)
        prod[j, 1, b] = out[:, W:].reshape(RING, RING, SHARE, W)

    def part(g, j, b, pos):
        return prod.at[j, 0, b, :, pos] if g == 0 else prod.at[j, 1, b, pos]

    def step1(j, b):
        d = 1 if b < 2 else -1
        for g in (0, 1):
            send(part(g, j, b, ring_pos(g, 2 * d)), r1.at[j, g, b, 0], ss1.at[j, g, b, 0], rs1.at[j, g, b, 0], ring_device(g, d))
            send(part(g, j, b, ring_pos(g, -d)), r1.at[j, g, b, 2], ss1.at[j, g, b, 2], rs1.at[j, g, b, 2], ring_device(g, -d))

    def step2(j, b):
        d = 1 if b < 2 else -1
        for g in (0, 1):
            wait_recv(r1.at[j, g, b, 0], ss1.at[j, g, b, 0], rs1.at[j, g, b, 0])
            own = part(g, j, b, ring_pos(g, d))[...]
            f1[j, g, b] = (own.astype(F32) + r1[j, g, b, 0].astype(F32)).astype(BF16)
            send(f1.at[j, g, b], r1.at[j, g, b, 1], ss1.at[j, g, b, 1], rs1.at[j, g, b, 1], ring_device(g, d))

    def final1(j, b):
        for g in (0, 1):
            for t in (1, 2):
                wait_recv(r1.at[j, g, b, t], ss1.at[j, g, b, t], rs1.at[j, g, b, t])
            own = part(g, j, b, ring_pos(g, 0))[...]
            q[j, g, b] = (own.astype(F32) + r1[j, g, b, 1].astype(F32) + r1[j, g, b, 2].astype(F32)).astype(BF16)

    def part2(g, j, h, pos):
        return q.at[j, g, pl.ds(2 * h, 2), pos]

    def step3(j, h):
        d = 1 if h == 0 else -1
        for g in (0, 1):
            a = 1 - g
            send(part2(g, j, h, ring_pos(a, 2 * d)), r2.at[j, g, h, 0], ss2.at[j, g, h, 0], rs2.at[j, g, h, 0], ring_device(a, d))
            send(part2(g, j, h, ring_pos(a, -d)), r2.at[j, g, h, 2], ss2.at[j, g, h, 2], rs2.at[j, g, h, 2], ring_device(a, -d))

    def step4(j, h):
        d = 1 if h == 0 else -1
        for g in (0, 1):
            a = 1 - g
            wait_recv(r2.at[j, g, h, 0], ss2.at[j, g, h, 0], rs2.at[j, g, h, 0])
            own = part2(g, j, h, ring_pos(a, d))[...]
            f2[j, g, h] = (own.astype(F32) + r2[j, g, h, 0].astype(F32)).astype(BF16)
            send(f2.at[j, g, h], r2.at[j, g, h, 1], ss2.at[j, g, h, 1], rs2.at[j, g, h, 1], ring_device(a, d))

    def final2(j):
        for h in (0, 1):
            for g in (0, 1):
                a = 1 - g
                for t in (1, 2):
                    wait_recv(r2.at[j, g, h, t], ss2.at[j, g, h, t], rs2.at[j, g, h, t])
                own = part2(g, j, h, ring_pos(a, 0))[...]
                total = own.astype(F32) + r2[j, g, h, 1].astype(F32) + r2[j, g, h, 2].astype(F32)
                for i in (0, 1):
                    b = 2 * h + i
                    size = size_s[b]
                    live = (m * SHARE + iota((SHARE, W), 0) < size) & (g * 256 + j * W + iota((SHARE, W), 1) < size)
                    pieces[j, g * NB + b] = jnp.where(live, total[i], 0.0).astype(BF16)
        packed = jnp.dot(place[...], pieces[j].reshape(256, W), preferred_element_type=F32).astype(BF16)
        sbuf[j] = packed.reshape(NS, SLOT_ROWS, W)
        own_copy = pltpu.make_async_copy(sbuf.at[j, s], arr.at[j, s], rsb.at[j])
        own_copy.start()

        @pl.loop(1, NS)
        def _(i):
            peer = (s + peer_offset(i)) % NS
            pltpu.make_async_remote_copy(
                src_ref=sbuf.at[j, peer], dst_ref=arr.at[j, s], send_sem=ssb.at[j], recv_sem=rsb.at[j],
                device_id={"mpo": m, "sector": peer}, device_id_type=MESH,
            ).start()

    def peer_offset(i):
        return NS // 2 + (1 - 2 * (i % 2)) * (i // 2) + 0 * i

    def collect_chunk(j):
        pltpu.make_async_copy(arr.at[j], arr.at[j], rsb.at[j]).wait()
        got = arr[j].reshape(NS * SLOT_ROWS, W)
        res = lax.dot_general(collect[...], got, (((0,), (0,)), ((), ())), preferred_element_type=F32).astype(BF16)
        for c in (0, 1):
            outv[:, :, c * 256 + j * W : c * 256 + (j + 1) * W] = res[c * 128 : (c + 1) * 128].reshape(NB, SHARE, W)

    def make_row():
        lane = iota((1, 128), 1)
        acc = jnp.full((1, 128), 4 * NS, I32)
        for b in range(NB):
            for k in range(8):
                acc = jnp.where(lane == b * 8 + k, owner_s[0, b, k] * 4 + block_s[0, b, k], acc)
        row[...] = acc

    def send_rows():
        pltpu.make_async_copy(row, tab.at[s], rsm).start()

        @pl.loop(1, NS)
        def _(i):
            peer = (s + peer_offset(i)) % NS
            pltpu.make_async_remote_copy(
                src_ref=row, dst_ref=tab.at[s], send_sem=ssm, recv_sem=rsm,
                device_id={"mpo": m, "sector": peer}, device_id_type=MESH,
            ).start()

    lane_p = iota((NS, 128), 1)
    base_of = (lane_p % 2) * 128 + ((lane_p // 2) % 4) * 8

    def make_place():
        table = jnp.broadcast_to(row[...], (NS, 128))
        chosen = table // 4 == iota((NS, 128), 0)
        place[...] = one_hot_rows(chosen, base_of + (lane_p // 8) * 32)

    def make_collect():
        pltpu.make_async_copy(tab, tab, rsm).wait()
        table = tab[...].reshape(NS, 128)
        chosen = table // 4 == s
        collect[...] = one_hot_rows(chosen, base_of + (table % 4) * 32)

    make_row()
    compute(0, 0)
    pl.semaphore_wait(barrier, 4 + NS - 1)
    step1(0, 0)
    send_rows()
    for b in range(1, NB):
        compute(0, b)
        step1(0, b)
    make_place()
    compute(1, 0)
    step1(1, 0)
    step2(0, 0)
    compute(1, 1)
    step1(1, 1)
    step2(0, 1)
    compute(1, 2)
    step1(1, 2)
    step2(0, 2)
    final1(0, 0)
    final1(0, 1)
    step3(0, 0)
    compute(1, 3)
    step1(1, 3)
    step2(0, 3)
    final1(0, 2)
    final1(0, 3)
    step3(0, 1)
    step2(1, 0)
    make_collect()
    step4(0, 0)
    step2(1, 1)
    step4(0, 1)
    step2(1, 2)
    final2(0)
    step2(1, 3)
    final1(1, 0)
    final1(1, 1)
    step3(1, 0)
    final1(1, 2)
    final1(1, 3)
    step3(1, 1)
    step4(1, 0)
    step4(1, 1)
    final2(1)
    collect_chunk(0)
    collect_chunk(1)
    copy_out = pltpu.make_async_copy(outv, out_ref, out_sem)
    copy_out.start()
    for c in started:
        c.wait_send()
    for j in range(CHUNKS):
        pltpu.make_async_copy(arr.at[j, pl.ds(0, NS - 1)], arr.at[j, pl.ds(0, NS - 1)], ssb.at[j]).wait()
    pltpu.make_async_copy(tab.at[pl.ds(0, NS - 1)], tab.at[pl.ds(0, NS - 1)], ssm).wait()
    copy_out.wait()


def per_device(wavefunction, left_env, right_env, mpo_mask, block_size, route_owner, route_block):
    anyspec = pl.BlockSpec(memory_space=pl.ANY)
    dma = pltpu.SemaphoreType.DMA
    return pl.pallas_call(
        kernel,
        out_shape=jax.ShapeDtypeStruct((NB, SHARE, N), BF16),
        in_specs=[anyspec] * 7,
        out_specs=anyspec,
        scratch_shapes=[
            pltpu.VMEM((NB, N, N), BF16),
            pltpu.VMEM((NB, N, N), BF16),
            pltpu.VMEM((NB, N, N), BF16),
            pltpu.VMEM((CHUNKS, 2, NB, RING, RING, SHARE, W), BF16),
            pltpu.VMEM((CHUNKS, 2, NB, 3, RING, SHARE, W), BF16),
            pltpu.VMEM((CHUNKS, 2, NB, RING, SHARE, W), BF16),
            pltpu.VMEM((CHUNKS, 2, NB, RING, SHARE, W), BF16),
            pltpu.VMEM((CHUNKS, 2, 2, 3, 2, SHARE, W), BF16),
            pltpu.VMEM((CHUNKS, 2, 2, 2, SHARE, W), BF16),
            pltpu.VMEM((CHUNKS, 2 * NB, SHARE, W), BF16),
            pltpu.VMEM((CHUNKS, NS, SLOT_ROWS, W), BF16),
            pltpu.VMEM((CHUNKS, NS, SLOT_ROWS, W), BF16),
            pltpu.VMEM((NS, 1, 128), I32),
            pltpu.VMEM((1, 128), I32),
            pltpu.VMEM((NS * SLOT_ROWS, 256), BF16),
            pltpu.VMEM((NS * SLOT_ROWS, 256), BF16),
            pltpu.VMEM((NB, SHARE, N), BF16),
            pltpu.SMEM((1, NB), I32),
            pltpu.SMEM((NB,), I32),
            pltpu.SMEM((1, NB, 8), I32),
            pltpu.SMEM((1, NB, 8), I32),
            dma((NB, 3)),
            dma((4,)),
            dma((CHUNKS, 2, NB, 3)),
            dma((CHUNKS, 2, NB, 3)),
            dma((CHUNKS, 2, 2, 3)),
            dma((CHUNKS, 2, 2, 3)),
            dma((CHUNKS,)),
            dma((CHUNKS,)),
            dma,
            dma,
            dma,
        ],
        compiler_params=pltpu.CompilerParams(collective_id=0, has_side_effects=True, vmem_limit_bytes=67043328),
    )(wavefunction, left_env, right_env, mpo_mask, block_size, route_owner, route_block)


def solution(mesh):
    placed = (
        P("sector", None, None),
        P("mpo", "sector", None, None),
        P("mpo", "sector", None, None),
        P("mpo", "sector"),
        P("sector"),
        P("mpo", "sector", None),
        P("mpo", "sector", None),
    )
    return jax.shard_map(per_device, mesh=mesh, in_specs=placed, out_specs=P("sector", "mpo", None), check_vma=False)
```

```python
import jax
import jax.numpy as jnp
from jax import lax
from jax.experimental import pallas as pl
from jax.experimental.pallas import tpu as pltpu
from jax.sharding import PartitionSpec as P

MESH = pl.DeviceIdType.MESH
F32, BF16, I32 = jnp.float32, jnp.bfloat16, jnp.int32
NB = 4
N = 512
RING = 4
SHARE = 32
CHUNKS = 4
CW = 64
W = 128
NS = 32
PR = 8

GROUPS = ((0, (0,)), (0, (2,)), (0, (1, 3)), (1, (0, 2)), (1, (1, 3)))
ORDER = (
    ("C", 0, 0), ("S1", 0, 0), ("C", 1, 0), ("S1", 1, 2), ("P", 0, 0), ("S1", 0, 2), ("S1", 1, 0), ("Z", 1, 0),
    ("C", 2, 0), ("S1", 0, 1), ("S1", 0, 3), ("S1", 1, 3), ("S1", 1, 1), ("Z", 2, 0), ("C", 3, 0), ("F1", 0, 0),
    ("F1", 1, 2), ("S1", 2, 0), ("Z", 3, 0), ("S1", 2, 2), ("C", 4, 0), ("F1", 0, 2), ("F1", 0, 1), ("F1", 0, 3),
    ("S1", 2, 1), ("S1", 2, 3), ("F1", 1, 0), ("Z", 4, 0), ("F1", 1, 1), ("F1", 1, 3), ("Z", 5, 0), ("S1", 3, 1),
    ("F2", 0, 0), ("F2", 1, 2), ("S1", 3, 2), ("S1", 3, 0), ("S1", 3, 3), ("F1", 2, 0), ("F2", 0, 2), ("F1", 2, 2),
    ("F2", 0, 3), ("F2", 0, 1), ("B", 0, 0), ("F1", 2, 1), ("F1", 2, 3), ("F2", 1, 3), ("F2", 1, 0), ("F2", 1, 1),
    ("B", 1, 0), ("F1", 3, 1), ("F1", 3, 2), ("F1", 3, 0), ("F1", 3, 3), ("F2", 2, 3), ("F2", 2, 2), ("F2", 2, 0),
    ("F2", 2, 1), ("B", 2, 0), ("F2", 3, 1), ("F2", 3, 2), ("F2", 3, 0), ("F2", 3, 3), ("B", 3, 0), ("Q", 0, 0),
    ("K", 0, 0), ("K", 1, 0), ("K", 2, 0), ("K", 3, 0),
)


def iota(shape, dim):
    return lax.broadcasted_iota(I32, shape, dim)


def one_hot_rows(chosen, base):
    lane = iota((NS, 128), 1)
    first = jnp.min(jnp.where(chosen, lane, 999), axis=1, keepdims=True)
    last = jnp.max(jnp.where(chosen, lane, -1), axis=1, keepdims=True)
    at_first = jnp.sum(jnp.where(lane == first, base, 0), axis=1, keepdims=True).astype(F32)
    at_last = jnp.sum(jnp.where(lane == last, base, 0), axis=1, keepdims=True).astype(F32)
    slot0 = jnp.where(first < 999, at_first, 256.0)
    slot1 = jnp.where(last > first, at_last, 256.0)
    both = jnp.where(lane < 64, slot0, slot1).astype(BF16)
    spread = (iota((NS * PR, NS), 0) // PR == iota((NS * PR, NS), 1)).astype(F32).astype(BF16)
    rows = jnp.dot(spread, both, preferred_element_type=F32)
    inner = iota((NS * PR, 1), 0) % PR
    out = []
    for at in (0, 64):
        value = rows[:, at : at + 1].astype(I32)
        value = jnp.where(value < 256, value + inner, -1)
        out.append((iota((NS * PR, 256), 1) == value).astype(F32))
    return out


def kernel(
    wf_hbm, le_hbm, re_hbm, mask_hbm, size_hbm, owner_hbm, block_hbm,
    out_ref,
    wf, le, re, prod, r1, q, r2, pieces, sbuf, arr, tab, row, place, collect, half,
    mask_s, size_s, owner_s, block_s,
    load_sem, small_sem, ss1, rs1, ss2, rs2, ssb, rsb, ssm, rsm, news,
):
    m = lax.axis_index("mpo")
    s = lax.axis_index("sector")
    y, x = m // RING, m % RING
    loads = {}

    def load(key, src, dst, sem):
        c = pltpu.make_async_copy(src, dst, sem)
        c.start()
        loads[key] = c

    def ring_device(axis, delta):
        if axis == 0:
            return y * RING + (x + delta + RING) % RING
        return ((y + delta + RING) % RING) * RING + x

    def ring_pos(axis, delta):
        return ((x if axis == 0 else y) + delta + RING) % RING

    def tell(sem, dev, sector):
        pl.semaphore_signal(sem, inc=1, device_id={"mpo": dev, "sector": sector}, device_id_type=MESH)

    partner = s + 1 - 2 * (s % 2)
    barrier = pltpu.get_barrier_semaphore()
    for axis in (0, 1):
        for delta in (1, -1, 2):
            tell(barrier, ring_device(axis, delta), s)
    tell(barrier, m, (s + 2) % NS)
    tell(barrier, m, (s + NS - 2) % NS)
    tell(barrier, m, partner)

    load("mask", mask_hbm, mask_s, small_sem.at[0])
    load("size", size_hbm, size_s, small_sem.at[1])
    for b in (0, 2, 1, 3):
        load(("wf", b), wf_hbm.at[b], wf.at[b], load_sem.at[b, 0])
        load(("re", b, 0), re_hbm.at[0, b, pl.ds(0, W)], re.at[b, pl.ds(0, W)], load_sem.at[b, 1])
        load(("re", b, 1), re_hbm.at[0, b, pl.ds(256, W)], re.at[b, pl.ds(256, W)], load_sem.at[b, 2])
        load(("le", b), le_hbm.at[0, b], le.at[b], load_sem.at[b, 3])
    load("owner", owner_hbm, owner_s, small_sem.at[2])
    load("block", block_hbm, block_s, small_sem.at[3])
    for b in (0, 2, 1, 3):
        load(("re", b, 2), re_hbm.at[0, b, pl.ds(W, W)], re.at[b, pl.ds(W, W)], load_sem.at[b, 4])
        load(("re", b, 3), re_hbm.at[0, b, pl.ds(256 + W, W)], re.at[b, pl.ds(256 + W, W)], load_sem.at[b, 5])
    loads["mask"].wait()
    loads["size"].wait()

    started = []

    def send(src, dst, ss, rs, dev):
        c = pltpu.make_async_remote_copy(
            src_ref=src, dst_ref=dst, send_sem=ss, recv_sem=rs, device_id={"mpo": dev, "sector": s}, device_id_type=MESH
        )
        c.start()
        started.append(c)

    def arrived(dst, ss, rs):
        pltpu.make_async_remote_copy(
            src_ref=dst, dst_ref=dst, send_sem=ss, recv_sem=rs, device_id={"mpo": m, "sector": s}, device_id_type=MESH
        ).wait_recv()

    entered = [False]

    def compute(group):
        jp, blocks = GROUPS[group]
        rights = []
        for b in blocks:
            size = size_s[b] * mask_s[0, b]
            if jp == 0:
                loads[("wf", b)].wait()
                live = (iota((1, N), 1) < size).astype(F32).astype(BF16)
                wf[b] = wf[b] * live
            loads[("re", b, 2 * jp)].wait()
            loads[("re", b, 2 * jp + 1)].wait()
            if jp == 0:
                loads[("le", b)].wait()
        for b in blocks:
            size = size_s[b] * mask_s[0, b]
            rhs = jnp.concatenate(
                [re[b, c * 256 + (2 * jp + h) * CW : c * 256 + (2 * jp + h + 1) * CW] for h in (0, 1) for c in (0, 1)],
                axis=0,
            )
            right = lax.dot_general(wf[b], rhs, (((1,), (1,)), ((), ())), preferred_element_type=F32)
            rights.append(jnp.where(iota((N, 1), 0) < size, right, 0.0).astype(BF16))
        for b, right in zip(blocks, rights):
            out = jnp.dot(le[b], right, preferred_element_type=F32).astype(BF16)
            for h in (0, 1):
                prod[2 * jp + h, b] = out[:, h * W : (h + 1) * W].reshape(RING, RING, SHARE, W)

    def axis_of(b):
        return 0 if b < 2 else 1

    def part(j, b, pos):
        return prod.at[j, b, :, pos] if axis_of(b) == 0 else prod.at[j, b, pos]

    def step1(j, b):
        if not entered[0]:
            entered[0] = True
            pl.semaphore_wait(barrier, 9)
        a = axis_of(b)
        for t, d in ((0, 2), (1, 1), (2, -1)):
            send(part(j, b, ring_pos(a, d)), r1.at[j, b, t], ss1.at[j, b, t], rs1.at[j, b, t], ring_device(a, d))

    def final1(j, b):
        a = axis_of(b)
        for t in (1, 2, 0):
            arrived(r1.at[j, b, t], ss1.at[j, b, t], rs1.at[j, b, t])
        total = part(j, b, ring_pos(a, 0))[...].astype(F32)
        for t in (0, 1, 2):
            total = total + r1[j, b, t].astype(F32)
        q[j, b] = total.astype(BF16)
        a = 1 - a
        for t, d in ((0, 2), (1, 1), (2, -1)):
            send(q.at[j, b, ring_pos(a, d)], r2.at[j, b, t], ss2.at[j, b, t], rs2.at[j, b, t], ring_device(a, d))

    def final2(j, b):
        a = 1 - axis_of(b)
        for t in (1, 2, 0):
            arrived(r2.at[j, b, t], ss2.at[j, b, t], rs2.at[j, b, t])
        total = q[j, b, ring_pos(a, 0)].astype(F32)
        for t in (0, 1, 2):
            total = total + r2[j, b, t].astype(F32)
        lane = iota((SHARE, W), 1)
        column = (lane // CW) * 256 + j * CW + lane % CW
        live = (m * SHARE + iota((SHARE, W), 0) < size_s[b]) & (column < size_s[b])
        pieces[j, b] = jnp.where(live, total, 0.0)

    def peer_at(i):
        return (s + NS // 2 + (1 - 2 * (i % 2)) * (i // 2)) % NS

    def to_peers(src_of, dst, ss, rs):
        @pl.loop(1, NS)
        def _(i):
            peer = peer_at(i)
            pltpu.make_async_remote_copy(
                src_ref=src_of(peer), dst_ref=dst, send_sem=ss, recv_sem=rs,
                device_id={"mpo": m, "sector": peer}, device_id_type=MESH,
            ).start()

    low = iota((NB * SHARE, W), 1) < CW

    def exchange(j):
        share = pieces[j].reshape(NB * SHARE, W)
        turned = pltpu.roll(share, CW, 1)
        rhs = jnp.concatenate([jnp.where(low, share, turned), jnp.where(low, turned, share)], axis=0).astype(BF16)
        slot0 = jnp.dot(place[0], rhs, preferred_element_type=F32)
        slot1 = jnp.dot(place[1], rhs, preferred_element_type=F32)
        packed = jnp.where(iota((NS * PR, W), 1) < CW, slot0, slot1).astype(BF16)
        sbuf[j] = packed.reshape(NS, PR, W)
        pltpu.make_async_copy(sbuf.at[j, s], arr.at[j, s], rsb.at[j]).start()
        to_peers(lambda peer: sbuf.at[j, peer], arr.at[j, s], ssb.at[j], rsb.at[j])

    def collect_chunk(j):
        pltpu.make_async_copy(arr.at[j], arr.at[j], rsb.at[j]).wait()
        got = arr[j].reshape(NS * PR, W)
        slot0 = jnp.dot(collect[0], got, preferred_element_type=F32)
        slot1 = jnp.dot(collect[1], got, preferred_element_type=F32)
        if j % 2 == 0:
            half[...] = slot0 + pltpu.roll(slot1, CW, 1)
        else:
            both = jnp.where(iota((NS * PR, W), 1) < CW, half[...], slot1 + pltpu.roll(slot0, CW, 1)).astype(BF16)
            for c in (0, 1):
                at = c * 256 + (j // 2) * W
                out_ref[:, :, at : at + W] = both[c * 128 : (c + 1) * 128].reshape(NB, SHARE, W)

    lane_p = iota((NS, 128), 1)
    base_of = (lane_p % 2) * 128 + ((lane_p // 2) % 4) * PR

    def make_place():
        loads["owner"].wait()
        loads["block"].wait()
        lane = iota((1, 128), 1)
        acc = jnp.full((1, 128), 4 * NS, I32)
        for b in range(NB):
            for k in range(8):
                acc = jnp.where(lane == b * 8 + k, owner_s[0, b, k] * 4 + block_s[0, b, k], acc)
        row[...] = acc
        table = jnp.broadcast_to(acc, (NS, 128))
        chosen = table // 4 == iota((NS, 128), 0)
        for t, one_hot in enumerate(one_hot_rows(chosen, base_of + (lane_p // 8) * SHARE)):
            place[t] = one_hot.astype(BF16)

    def make_collect():
        pltpu.make_async_copy(tab, tab, rsm).wait()
        table = tab[...].reshape(NS, 128)
        chosen = table // 4 == s
        for t, one_hot in enumerate(one_hot_rows(chosen, base_of + (table % 4) * SHARE)):
            collect[t] = one_hot.T.astype(BF16)

    def sector_news(i):
        if i <= 3:
            if i >= 2:
                pl.semaphore_wait(news.at[i - 2], 2)
            step = 2 ** i
            tell(news.at[i - 1], m, (s + step) % NS)
            tell(news.at[i - 1], m, (s + NS - step) % NS)
        elif i == 4:
            pl.semaphore_wait(news.at[2], 2)
            tell(news.at[3], m, partner)
        else:
            pl.semaphore_wait(news.at[3], 1)
            pltpu.make_async_copy(row, tab.at[s], rsm).start()
            to_peers(lambda peer: row, tab.at[s], ssm, rsm)

    for name, j, b in ORDER:
        if name == "C":
            compute(j)
        elif name == "S1":
            step1(j, b)
        elif name == "F1":
            final1(j, b)
        elif name == "F2":
            final2(j, b)
        elif name == "B":
            exchange(j)
        elif name == "K":
            collect_chunk(j)
        elif name == "P":
            make_place()
        elif name == "Q":
            make_collect()
        else:
            sector_news(j)
    for c in started:
        c.wait_send()
    for j in range(CHUNKS):
        pltpu.make_async_copy(arr.at[j, pl.ds(0, NS - 1)], arr.at[j, pl.ds(0, NS - 1)], ssb.at[j]).wait()
    pltpu.make_async_copy(tab.at[pl.ds(0, NS - 1)], tab.at[pl.ds(0, NS - 1)], ssm).wait()


def per_device(wavefunction, left_env, right_env, mpo_mask, block_size, route_owner, route_block):
    in_hbm = pl.BlockSpec(memory_space=pltpu.HBM)
    dma = pltpu.SemaphoreType.DMA
    vmem = pltpu.VMEM
    return pl.pallas_call(
        kernel,
        out_shape=jax.ShapeDtypeStruct((NB, SHARE, N), BF16),
        in_specs=[in_hbm] * 7,
        out_specs=pl.BlockSpec(memory_space=pltpu.VMEM),
        scratch_shapes=[
            vmem((NB, N, N), BF16),
            vmem((NB, N, N), BF16),
            vmem((NB, N, N), BF16),
            vmem((CHUNKS, NB, RING, RING, SHARE, W), BF16),
            vmem((CHUNKS, NB, 3, RING, SHARE, W), BF16),
            vmem((CHUNKS, NB, RING, SHARE, W), BF16),
            vmem((CHUNKS, NB, 3, SHARE, W), BF16),
            vmem((CHUNKS, NB, SHARE, W), F32),
            vmem((CHUNKS, NS, PR, W), BF16),
            vmem((CHUNKS, NS, PR, W), BF16),
            vmem((NS, 1, 128), I32),
            vmem((1, 128), I32),
            vmem((2, NS * PR, 256), BF16),
            vmem((2, 256, NS * PR), BF16),
            vmem((256, W), F32),
            pltpu.SMEM((1, NB), I32),
            pltpu.SMEM((NB,), I32),
            pltpu.SMEM((1, NB, 8), I32),
            pltpu.SMEM((1, NB, 8), I32),
            dma((NB, 6)),
            dma((4,)),
            dma((CHUNKS, NB, 3)),
            dma((CHUNKS, NB, 3)),
            dma((CHUNKS, NB, 3)),
            dma((CHUNKS, NB, 3)),
            dma((CHUNKS,)),
            dma((CHUNKS,)),
            dma,
            dma,
            pltpu.SemaphoreType.REGULAR((4,)),
        ],
        compiler_params=pltpu.CompilerParams(collective_id=0, has_side_effects=True, vmem_limit_bytes=67043328),
    )(wavefunction, left_env, right_env, mpo_mask, block_size, route_owner, route_block)


def solution(mesh):
    placed = (
        P("sector", None, None),
        P("mpo", "sector", None, None),
        P("mpo", "sector", None, None),
        P("mpo", "sector"),
        P("sector"),
        P("mpo", "sector", None),
        P("mpo", "sector", None),
    )
    return jax.shard_map(per_device, mesh=mesh, in_specs=placed, out_specs=P("sector", "mpo", None), check_vma=False)
```

```python
import jax
import jax.numpy as jnp
from jax import lax
from jax.experimental import pallas as pl
from jax.experimental.pallas import tpu as pltpu
from jax.sharding import PartitionSpec as P

MESH = pl.DeviceIdType.MESH
F32, BF16, I32 = jnp.float32, jnp.bfloat16, jnp.int32
NB = 4
N = 512
RING = 4
SHARE = 32
CHUNKS = 4
CW = 64
W = 128
NS = 32
PR = 8

GROUPS = ((0, (0,)), (0, (2,)), (0, (1, 3)), (1, (0, 2)), (1, (1, 3)))
ORDER = (
    ("C", 0, 0), ("S1", 0, 0), ("C", 1, 0), ("S1", 1, 2), ("P", 0, 0), ("S1", 0, 2), ("S1", 1, 0), ("Z", 1, 0),
    ("C", 2, 0), ("S1", 0, 1), ("S1", 0, 3), ("S1", 1, 3), ("S1", 1, 1), ("Z", 2, 0), ("C", 3, 0), ("F1", 0, 0),
    ("F1", 1, 2), ("S1", 2, 0), ("Z", 3, 0), ("S1", 2, 2), ("C", 4, 0), ("F1", 0, 2), ("F1", 0, 1), ("F1", 0, 3),
    ("S1", 2, 1), ("S1", 2, 3), ("F1", 1, 0), ("Z", 4, 0), ("F1", 1, 1), ("F1", 1, 3), ("Z", 5, 0), ("S1", 3, 1),
    ("F2", 0, 0), ("F2", 1, 2), ("S1", 3, 2), ("S1", 3, 0), ("S1", 3, 3), ("F1", 2, 0), ("F2", 0, 2), ("F1", 2, 2),
    ("F2", 0, 3), ("F2", 0, 1), ("B", 0, 0), ("F1", 2, 1), ("F1", 2, 3), ("F2", 1, 3), ("F2", 1, 0), ("F2", 1, 1),
    ("B", 1, 0), ("F1", 3, 1), ("F1", 3, 2), ("F1", 3, 0), ("F1", 3, 3), ("F2", 2, 3), ("F2", 2, 2), ("F2", 2, 0),
    ("F2", 2, 1), ("B", 2, 0), ("F2", 3, 1), ("F2", 3, 2), ("F2", 3, 0), ("F2", 3, 3), ("B", 3, 0), ("Q", 0, 0),
    ("K", 0, 0), ("K", 1, 0), ("K", 2, 0), ("K", 3, 0),
)


def iota(shape, dim):
    return lax.broadcasted_iota(I32, shape, dim)


def one_hot_rows(chosen, base):
    lane = iota((NS, 128), 1)
    first = jnp.min(jnp.where(chosen, lane, 999), axis=1, keepdims=True)
    last = jnp.max(jnp.where(chosen, lane, -1), axis=1, keepdims=True)
    at_first = jnp.sum(jnp.where(lane == first, base, 0), axis=1, keepdims=True).astype(F32)
    at_last = jnp.sum(jnp.where(lane == last, base, 0), axis=1, keepdims=True).astype(F32)
    slot0 = jnp.where(first < 999, at_first, 256.0)
    slot1 = jnp.where(last > first, at_last, 256.0)
    both = jnp.where(lane < 64, slot0, slot1).astype(BF16)
    spread = (iota((NS * PR, NS), 0) // PR == iota((NS * PR, NS), 1)).astype(F32).astype(BF16)
    rows = jnp.dot(spread, both, preferred_element_type=F32)
    inner = iota((NS * PR, 1), 0) % PR
    out = []
    for at in (0, 64):
        value = rows[:, at : at + 1].astype(I32)
        value = jnp.where(value < 256, value + inner, -1)
        out.append((iota((NS * PR, 256), 1) == value).astype(F32))
    return out


def kernel(
    wf_hbm, le_hbm, re_hbm, mask_hbm, size_hbm, owner_hbm, block_hbm,
    out_ref,
    wf, le, re, prod, r1, q, r2, pieces, sbuf, arr, tab, row, place, collect, half,
    mask_s, size_s, owner_s, block_s,
    load_sem, small_sem, ss1, rs1, ss2, rs2, ssb, rsb, ssm, rsm, news,
):
    m = lax.axis_index("mpo")
    s = lax.axis_index("sector")
    y, x = lax.div(m, RING), lax.rem(m, RING)
    loads = {}

    def load(key, src, dst, sem):
        c = pltpu.make_async_copy(src, dst, sem)
        c.start()
        loads[key] = c

    def ring_device(axis, delta):
        if axis == 0:
            return y * RING + lax.rem(x + delta + RING, RING)
        return lax.rem(y + delta + RING, RING) * RING + x

    def ring_pos(axis, delta):
        return lax.rem((x if axis == 0 else y) + delta + RING, RING)

    def tell(sem, dev, sector):
        pl.semaphore_signal(sem, inc=1, device_id={"mpo": dev, "sector": sector}, device_id_type=MESH)

    for b in (0, 2, 1, 3):
        if b == 2:
            load("mask", mask_hbm, mask_s, small_sem.at[0])
            load("size", size_hbm, size_s, small_sem.at[1])
        load(("wf", b), wf_hbm.at[b], wf.at[b], load_sem.at[b, 0])
        load(("re", b, 0), re_hbm.at[0, b, pl.ds(0, W)], re.at[b, pl.ds(0, W)], load_sem.at[b, 1])
        load(("re", b, 1), re_hbm.at[0, b, pl.ds(256, W)], re.at[b, pl.ds(256, W)], load_sem.at[b, 2])
        load(("le", b), le_hbm.at[0, b], le.at[b], load_sem.at[b, 3])
    load("owner", owner_hbm, owner_s, small_sem.at[2])
    load("block", block_hbm, block_s, small_sem.at[3])
    for b in (0, 2, 1, 3):
        load(("re", b, 2), re_hbm.at[0, b, pl.ds(W, W)], re.at[b, pl.ds(W, W)], load_sem.at[b, 4])
        load(("re", b, 3), re_hbm.at[0, b, pl.ds(256 + W, W)], re.at[b, pl.ds(256 + W, W)], load_sem.at[b, 5])
    partner = s + 1 - 2 * lax.rem(s, 2)
    barrier = pltpu.get_barrier_semaphore()
    for axis in (0, 1):
        for delta in (1, -1, 2):
            tell(barrier, ring_device(axis, delta), s)
    tell(barrier, m, lax.rem(s + 2, NS))
    tell(barrier, m, lax.rem(s + NS - 2, NS))
    tell(barrier, m, partner)

    loads["mask"].wait()
    loads["size"].wait()

    started = []

    def send(src, dst, ss, rs, dev):
        c = pltpu.make_async_remote_copy(
            src_ref=src, dst_ref=dst, send_sem=ss, recv_sem=rs, device_id={"mpo": dev, "sector": s}, device_id_type=MESH
        )
        c.start()
        started.append(c)

    def arrived(dst, ss, rs):
        pltpu.make_async_remote_copy(
            src_ref=dst, dst_ref=dst, send_sem=ss, recv_sem=rs, device_id={"mpo": m, "sector": s}, device_id_type=MESH
        ).wait_recv()

    entered = [False]

    def compute(group):
        jp, blocks = GROUPS[group]
        rights = []
        for b in blocks:
            size = size_s[b] * mask_s[0, b]
            if jp == 0:
                loads[("wf", b)].wait()
                live = (iota((1, N), 1) < size).astype(F32).astype(BF16)
                wf[b] = wf[b] * live
            loads[("re", b, 2 * jp)].wait()
            loads[("re", b, 2 * jp + 1)].wait()
            if jp == 0:
                loads[("le", b)].wait()
        for b in blocks:
            size = size_s[b] * mask_s[0, b]
            rhs = jnp.concatenate(
                [re[b, c * 256 + (2 * jp + h) * CW : c * 256 + (2 * jp + h + 1) * CW] for h in (0, 1) for c in (0, 1)],
                axis=0,
            )
            right = lax.dot_general(wf[b], rhs, (((1,), (1,)), ((), ())), preferred_element_type=F32)
            rights.append(jnp.where(iota((N, 1), 0) < size, right, 0.0).astype(BF16))
        for b, right in zip(blocks, rights):
            out = jnp.dot(le[b], right, preferred_element_type=F32).astype(BF16)
            for h in (0, 1):
                prod[2 * jp + h, b] = out[:, h * W : (h + 1) * W].reshape(RING, RING, SHARE, W)

    def axis_of(b):
        return 0 if b < 2 else 1

    def part(j, b, pos):
        return prod.at[j, b, :, pos] if axis_of(b) == 0 else prod.at[j, b, pos]

    def step1(j, b):
        if not entered[0]:
            entered[0] = True
            pl.semaphore_wait(barrier, 9)
        a = axis_of(b)
        for t, d in ((0, 2), (1, 1), (2, -1)):
            send(part(j, b, ring_pos(a, d)), r1.at[j, b, t], ss1.at[j, b, t], rs1.at[j, b, t], ring_device(a, d))

    def final1(j, b):
        a = axis_of(b)
        for t in (1, 2, 0):
            arrived(r1.at[j, b, t], ss1.at[j, b, t], rs1.at[j, b, t])
        total = part(j, b, ring_pos(a, 0))[...].astype(F32)
        for t in (0, 1, 2):
            total = total + r1[j, b, t].astype(F32)
        q[j, b] = total.astype(BF16)
        a = 1 - a
        for t, d in ((0, 2), (1, 1), (2, -1)):
            send(q.at[j, b, ring_pos(a, d)], r2.at[j, b, t], ss2.at[j, b, t], rs2.at[j, b, t], ring_device(a, d))

    def final2(j, b):
        a = 1 - axis_of(b)
        for t in (1, 2, 0):
            arrived(r2.at[j, b, t], ss2.at[j, b, t], rs2.at[j, b, t])
        total = q[j, b, ring_pos(a, 0)].astype(F32)
        for t in (0, 1, 2):
            total = total + r2[j, b, t].astype(F32)
        lane = iota((SHARE, W), 1)
        column = (lane // CW) * 256 + j * CW + lane % CW
        live = (m * SHARE + iota((SHARE, W), 0) < size_s[b]) & (column < size_s[b])
        pieces[j, b] = jnp.where(live, total, 0.0)

    def to_peers(src_of, dst, ss, rs):
        for i in range(1, NS):
            peer = lax.rem(s + (NS // 2 + (i // 2 if i % 2 else -(i // 2))), NS)
            pltpu.make_async_remote_copy(
                src_ref=src_of(peer), dst_ref=dst, send_sem=ss, recv_sem=rs,
                device_id={"mpo": m, "sector": peer}, device_id_type=MESH,
            ).start()

    low = iota((NB * SHARE, W), 1) < CW

    def exchange(j):
        share = pieces[j].reshape(NB * SHARE, W)
        turned = pltpu.roll(share, CW, 1)
        rhs = jnp.concatenate([jnp.where(low, share, turned), jnp.where(low, turned, share)], axis=0).astype(BF16)
        slot0 = jnp.dot(place[0], rhs, preferred_element_type=F32)
        slot1 = jnp.dot(place[1], rhs, preferred_element_type=F32)
        packed = jnp.where(iota((NS * PR, W), 1) < CW, slot0, slot1).astype(BF16)
        sbuf[j] = packed.reshape(NS, PR, W)
        pltpu.make_async_copy(sbuf.at[j, s], arr.at[j, s], rsb.at[j]).start()
        to_peers(lambda peer: sbuf.at[j, peer], arr.at[j, s], ssb.at[j], rsb.at[j])

    def collect_chunk(j):
        pltpu.make_async_copy(arr.at[j], arr.at[j], rsb.at[j]).wait()
        got = arr[j].reshape(NS * PR, W)
        slot0 = jnp.dot(collect[0], got, preferred_element_type=F32)
        slot1 = jnp.dot(collect[1], got, preferred_element_type=F32)
        if j % 2 == 0:
            half[...] = slot0 + pltpu.roll(slot1, CW, 1)
        else:
            both = jnp.where(iota((NS * PR, W), 1) < CW, half[...], slot1 + pltpu.roll(slot0, CW, 1)).astype(BF16)
            for c in (0, 1):
                at = c * 256 + (j // 2) * W
                out_ref[:, :, at : at + W] = both[c * 128 : (c + 1) * 128].reshape(NB, SHARE, W)

    lane_p = iota((NS, 128), 1)
    base_of = (lane_p % 2) * 128 + ((lane_p // 2) % 4) * PR

    def make_place():
        loads["owner"].wait()
        loads["block"].wait()
        lane = iota((1, 128), 1)
        acc = jnp.full((1, 128), 4 * NS, I32)
        for b in range(NB):
            for k in range(8):
                acc = jnp.where(lane == b * 8 + k, owner_s[0, b, k] * 4 + block_s[0, b, k], acc)
        row[...] = acc
        table = jnp.broadcast_to(acc, (NS, 128))
        chosen = table // 4 == iota((NS, 128), 0)
        for t, one_hot in enumerate(one_hot_rows(chosen, base_of + (lane_p // 8) * SHARE)):
            place[t] = one_hot.astype(BF16)

    def make_collect():
        pltpu.make_async_copy(tab, tab, rsm).wait()
        table = tab[...].reshape(NS, 128)
        chosen = table // 4 == s
        for t, one_hot in enumerate(one_hot_rows(chosen, base_of + (table % 4) * SHARE)):
            collect[t] = one_hot.T.astype(BF16)

    def sector_news(i):
        if i <= 3:
            if i >= 2:
                pl.semaphore_wait(news.at[i - 2], 2)
            step = 2 ** i
            tell(news.at[i - 1], m, lax.rem(s + step, NS))
            tell(news.at[i - 1], m, lax.rem(s + NS - step, NS))
        elif i == 4:
            pl.semaphore_wait(news.at[2], 2)
            tell(news.at[3], m, partner)
        else:
            pl.semaphore_wait(news.at[3], 1)
            pltpu.make_async_copy(row, tab.at[s], rsm).start()
            to_peers(lambda peer: row, tab.at[s], ssm, rsm)

    for name, j, b in ORDER:
        if name == "C":
            compute(j)
        elif name == "S1":
            step1(j, b)
        elif name == "F1":
            final1(j, b)
        elif name == "F2":
            final2(j, b)
        elif name == "B":
            exchange(j)
        elif name == "K":
            collect_chunk(j)
        elif name == "P":
            make_place()
        elif name == "Q":
            make_collect()
        else:
            sector_news(j)
    for c in started:
        c.wait_send()
    for j in range(CHUNKS):
        pltpu.make_async_copy(arr.at[j, pl.ds(0, NS - 1)], arr.at[j, pl.ds(0, NS - 1)], ssb.at[j]).wait()
    pltpu.make_async_copy(tab.at[pl.ds(0, NS - 1)], tab.at[pl.ds(0, NS - 1)], ssm).wait()


def per_device(wavefunction, left_env, right_env, mpo_mask, block_size, route_owner, route_block):
    in_hbm = pl.BlockSpec(memory_space=pltpu.HBM)
    dma = pltpu.SemaphoreType.DMA
    vmem = pltpu.VMEM
    args = (wavefunction, left_env, right_env, mpo_mask, block_size, route_owner, route_block)
    held = [pltpu.with_memory_space_constraint(a, pltpu.HBM) for a in args]
    return pl.pallas_call(
        kernel,
        out_shape=jax.ShapeDtypeStruct((NB, SHARE, N), BF16),
        in_specs=[in_hbm] * 7,
        out_specs=pl.BlockSpec(memory_space=pltpu.VMEM),
        scratch_shapes=[
            vmem((NB, N, N), BF16),
            vmem((NB, N, N), BF16),
            vmem((NB, N, N), BF16),
            vmem((CHUNKS, NB, RING, RING, SHARE, W), BF16),
            vmem((CHUNKS, NB, 3, RING, SHARE, W), BF16),
            vmem((CHUNKS, NB, RING, SHARE, W), BF16),
            vmem((CHUNKS, NB, 3, SHARE, W), BF16),
            vmem((CHUNKS, NB, SHARE, W), F32),
            vmem((CHUNKS, NS, PR, W), BF16),
            vmem((CHUNKS, NS, PR, W), BF16),
            vmem((NS, 1, 128), I32),
            vmem((1, 128), I32),
            vmem((2, NS * PR, 256), BF16),
            vmem((2, 256, NS * PR), BF16),
            vmem((256, W), F32),
            pltpu.SMEM((1, NB), I32),
            pltpu.SMEM((NB,), I32),
            pltpu.SMEM((1, NB, 8), I32),
            pltpu.SMEM((1, NB, 8), I32),
            dma((NB, 6)),
            dma((4,)),
            dma((CHUNKS, NB, 3)),
            dma((CHUNKS, NB, 3)),
            dma((CHUNKS, NB, 3)),
            dma((CHUNKS, NB, 3)),
            dma((CHUNKS,)),
            dma((CHUNKS,)),
            dma,
            dma,
            pltpu.SemaphoreType.REGULAR((4,)),
        ],
        compiler_params=pltpu.CompilerParams(collective_id=0, has_side_effects=True, vmem_limit_bytes=48 << 20),
    )(*held)


def solution(mesh):
    placed = (
        P("sector", None, None),
        P("mpo", "sector", None, None),
        P("mpo", "sector", None, None),
        P("mpo", "sector"),
        P("sector"),
        P("mpo", "sector", None),
        P("mpo", "sector", None),
    )
    return jax.shard_map(per_device, mesh=mesh, in_specs=placed, out_specs=P("sector", "mpo", None), check_vma=False)
```
